32 devices in a mesh: space: 4 (over y, x), batch: 8 (over z, core).
Axes of the slice: x: 2, y: 2, z: 4, core: 2. Of those that a mesh axis runs over, the one named last changes fastest.
Arguments:
- pre_act: bfloat16 [8, 64, 4, 8, 128], P('batch', None, 'space'), may hold values from -6 to 6
- grad_out: bfloat16 [8, 128, 4, 8, 128], P('batch', None, 'space'), may hold values from -6 to 6
- weight: bfloat16 [27, 64, 128], replicated, may hold values from -0.109375 to 0.109375
Outputs:
- grad_in: bfloat16 [8, 64, 4, 8, 128], P('batch', None, 'space')
- weight_grad: float32 [221184], P(('space', 'batch'))
The draws below stay inside these ranges and needn't reach their ends.
All inputs are finite; a program needn't handle non-finite values.
Results may differ from the reference program's by a relative error of at most 0.001.
Values may be sent and summed in bfloat16 or wider, within the bound.
A program may use at most 64 MiB of HBM per device.

```python
import jax
import jax.numpy as jnp
from jax import lax

CIN = 64
COUT = 128
YC = 8
ZC = 128
SAMPLES = 8
NX = 4


def block_scale(stream_key, dims, pieces, least, high):
    loudness, own = 1.0, jax.random.fold_in(stream_key, 6)
    for dim, shards_of in pieces:
        draws = jnp.exp(jax.random.uniform(jax.random.fold_in(own, dim), (shards_of,), jnp.float32, least / len(pieces), high / len(pieces)))
        loudness = loudness * jnp.repeat(draws, dims[dim] // shards_of).reshape([-1 if axis == dim else 1 for axis in range(len(dims))])
    return loudness


def normal_values(key, extent, scale, most, pieces=(), dtype=jnp.bfloat16):
    values = jax.random.normal(key, extent, jnp.float32) * scale
    if len(pieces) > 0:
        values = block_scale(key, extent, pieces, -0.22, 0.18) * values
    return jnp.clip(values, min=-most, max=most).astype(dtype)


def setup_inputs(seed: int = 0) -> dict:
    key_list = jax.random.split(jax.random.key(seed), 4)
    return {
        "pre_act": normal_values(key_list[0], (SAMPLES, CIN, NX, YC, ZC), 1.0, 6.0, ((0, 8), (2, 4))),
        "grad_out": normal_values(key_list[1], (SAMPLES, COUT, NX, YC, ZC), 1.0, 6.0, ((0, 8), (2, 4))),
        "weight": normal_values(key_list[2], (27, CIN, COUT), (27 * COUT) ** -0.5, 0.109375),
    }


slope = 0.3

def reference(pre_act, grad_out, weight):
    factor = 1.0 / jnp.sqrt(jnp.float32(SAMPLES * NX * YC * ZC))
    kernel = weight.astype(jnp.float32)

    def per_sample(sample_pair):
        act_one, grad_one = sample_pair
        act_float = act_one.astype(jnp.float32)
        hidden = jnp.where(act_float > 0, act_float, slope * act_float).astype(jnp.bfloat16)
        hidden = lax.optimization_barrier(hidden).astype(jnp.float32)
        padded = jnp.pad(grad_one.astype(jnp.float32), ((0, 0), (1, 1), (1, 1), (1, 1)))
        grad_hidden = jnp.zeros((CIN, NX, YC, ZC), jnp.float32)
        tap_grads = []
        for tap in range(27):
            shift_x = tap // 9 - 1
            shift_y = tap // 3 % 3 - 1
            shift_z = tap % 3 - 1
            window = padded[:, 1 - shift_x:1 - shift_x + NX, 1 - shift_y:1 - shift_y + YC, 1 - shift_z:1 - shift_z + ZC]
            grad_hidden = grad_hidden + jnp.einsum('ic,cxyz->ixyz', kernel[tap], window, precision=lax.Precision.HIGHEST)
            tap_grads.append(jnp.einsum('ixyz,cxyz->ic', hidden, window, precision=lax.Precision.HIGHEST))
        grad_one_in = (grad_hidden * jnp.where(act_float > 0, 1.0, slope)).astype(jnp.bfloat16)
        return (grad_one_in, jnp.stack(tap_grads))
    grad_in, taps_all = lax.map(per_sample, (pre_act, grad_out))
    weight_grad = (lax.optimization_barrier(jnp.sum(taps_all, axis=0)) * factor).reshape(-1)
    return (grad_in, weight_grad)
```

```python
import functools

import jax
import jax.numpy as jnp
from jax import lax
from jax.experimental import pallas as pl
from jax.experimental.pallas import tpu as pltpu
from jax.sharding import PartitionSpec as P

slope = 0.3


def padded(block, sides, width):
    for axis, dim in sides:
        count = lax.axis_size(axis)
        forward = [(i, i + 1) for i in range(count - 1)]
        backward = [(target, source) for source, target in forward]
        low = lax.ppermute(
            lax.slice_in_dim(block, block.shape[dim] - width, None, axis=dim), axis, forward
        )
        high = lax.ppermute(lax.slice_in_dim(block, 0, width, axis=dim), axis, backward)
        block = jnp.concatenate([low, block, high], axis=dim)
    return block


def leaky(values):
    return jnp.where(values > 0, values, slope * values)


def on_device(pre_act, grad_out, weight):
    local_x = pre_act.shape[2]
    local_y = pre_act.shape[3]
    local_z = pre_act.shape[4]
    count = (
        pre_act.shape[0]
        * lax.axis_size("batch")
        * local_x
        * lax.axis_size("space")
        * local_y
        * local_z
    )
    factor = 1.0 / jnp.sqrt(jnp.float32(count))
    act_float = pre_act.astype(jnp.float32)
    yz_pad = ((0, 0), (0, 0), (0, 0), (1, 1), (1, 1))
    grad_hidden = jnp.zeros(pre_act.shape, jnp.float32)
    tap_grads = []
    joined = jnp.concatenate([pre_act, grad_out], axis=1)
    widened = padded(joined, (("space", 2),), 1)
    in_chan = pre_act.shape[1]
    hidden_pad = jnp.pad(
        leaky(widened[:, :in_chan].astype(jnp.float32)).astype(jnp.bfloat16), yz_pad
    )
    grad_pad = jnp.pad(widened[:, in_chan:], yz_pad)
    for tap in range(27):
        shift_x = tap // 9 - 1
        shift_y = tap // 3 % 3 - 1
        shift_z = tap % 3 - 1
        window = grad_pad[
            :,
            :,
            1 - shift_x : 1 - shift_x + local_x,
            1 - shift_y : 1 - shift_y + local_y,
            1 - shift_z : 1 - shift_z + local_z,
        ]
        grad_hidden = grad_hidden + jnp.einsum(
            "ic,scxyz->sixyz", weight[tap], window, preferred_element_type=jnp.float32
        )
        moved = hidden_pad[
            :,
            :,
            1 + shift_x : 1 + shift_x + local_x,
            1 + shift_y : 1 + shift_y + local_y,
            1 + shift_z : 1 + shift_z + local_z,
        ]
        tap_grads.append(
            jnp.einsum("sixyz,scxyz->ic", moved, grad_out, preferred_element_type=jnp.float32)
        )
    grad_in = (grad_hidden * jnp.where(act_float > 0, 1.0, slope)).astype(jnp.bfloat16)
    partial_sum = (jnp.stack(tap_grads) * factor).reshape(-1)
    space_part = lax.psum_scatter(partial_sum, "space", scatter_dimension=0, tiled=True)
    weight_grad = lax.psum_scatter(space_part, "batch", scatter_dimension=0, tiled=True)
    return (grad_in, weight_grad)


MESH = pl.DeviceIdType.MESH


def prepare(values, scratch, target):
    channels, rows, lanes = values.shape
    scratch[0 : channels * rows, :] = values.reshape(channels * rows, lanes)
    lane = lax.broadcasted_iota(jnp.int32, (channels, lanes), 1)
    blank = jnp.zeros((3 * channels, lanes), target.dtype)
    target[:, 0:lanes] = blank
    target[:, (rows + 1) * lanes : (rows + 2) * lanes] = blank
    for row in range(rows):
        block = scratch[pl.ds(row, channels, stride=rows), :]
        before = jnp.where(lane == 0, 0.0, pltpu.roll(block, 1, 1))
        after = jnp.where(lane == lanes - 1, 0.0, pltpu.roll(block, lanes - 1, 1))
        for place, shifted in enumerate((before, block, after)):
            target[
                place * channels : (place + 1) * channels, (row + 1) * lanes : (row + 2) * lanes
            ] = shifted.astype(target.dtype)


def kernel(
    sizes,
    factor,
    scatter,
    pre_ref,
    grad_ref,
    weight_hbm,
    grad_in_ref,
    weight_grad_ref,
    pre_halo,
    grad_halo,
    weight_ref,
    plane,
    hidden_rows,
    grad_rows,
    total,
    partial,
    halo_send,
    halo_recv,
    weight_sem,
    *stage_refs,
):
    space_count, batch_count = sizes
    space, batch = lax.axis_index("space"), lax.axis_index("batch")
    channels, rows, lanes = pre_ref.shape
    cells = rows * lanes

    coords = dict(c=lax.rem(batch, 2), z=batch // 2, x=lax.rem(space, 2), y=space // 2)
    extents = dict(c=2, z=batch_count // 2, x=2, y=space_count // 2)

    def peer(axis, place):
        moved = dict(coords, **{axis: place})
        return (moved["y"] * 2 + moved["x"], moved["z"] * 2 + moved["c"])

    weight_copy = pltpu.make_async_copy(weight_hbm, weight_ref, weight_sem)
    weight_copy.start()

    has_left, has_right = space > 0, space < space_count - 1
    barrier = pltpu.get_barrier_semaphore()
    for there, condition in ((space - 1, has_left), (space + 1, has_right)):

        @pl.when(condition)
        def _():
            pl.semaphore_signal(barrier, inc=1, device_id=(there, batch), device_id_type=MESH)

    greeted = 0
    if scatter:
        for axis, extent in extents.items():
            for step in range(1, extent):
                pl.semaphore_signal(
                    barrier,
                    inc=1,
                    device_id=peer(axis, lax.rem(coords[axis] + step, extent)),
                    device_id_type=MESH,
                )
                greeted += 1
    beside = jnp.where(has_left, 1, 0) + jnp.where(has_right, 1, 0)
    pl.semaphore_wait(barrier, greeted + beside)

    def halo(source, slots, index, slot):
        there = space + 1 if slot == 0 else space - 1
        return pltpu.make_async_remote_copy(
            src_ref=source,
            dst_ref=slots.at[slot],
            send_sem=halo_send.at[index, slot],
            recv_sem=halo_recv.at[index, slot],
            device_id=(there, batch),
            device_id_type=MESH,
        )

    pairs = ((pre_ref, pre_halo), (grad_ref, grad_halo))
    for index, (source, slots) in enumerate(pairs):
        for slot, condition in ((0, has_right), (1, has_left)):

            @pl.when(condition)
            def _():
                halo(source, slots, index, slot).start()

    def arrive(index):
        source, slots = pairs[index]
        for slot, condition in ((0, has_left), (1, has_right)):

            @pl.when(condition)
            def _():
                halo(source, slots, index, slot).wait_recv()

            @pl.when(jnp.logical_not(condition))
            def _():
                slots[slot] = jnp.zeros(slots.shape[1:], slots.dtype)

    def hidden_plane(values, shift):
        prepare(leaky(values.astype(jnp.float32)), plane, hidden_rows.at[shift + 1])

    def grad_plane(values, shift):
        prepare(values.astype(jnp.float32), plane, grad_rows.at[shift + 1])

    out_chan = grad_ref.shape[0]

    def weight_terms(shift_x):
        own = grad_rows[1, out_chan : 2 * out_chan, lanes : lanes + cells]
        for shift_y in (-1, 0, 1):
            start = (9 * (shift_x + 1) + 3 * (shift_y + 1)) * channels
            term = lax.dot_general(
                hidden_rows[shift_x + 1, :, (1 + shift_y) * lanes : (1 + shift_y) * lanes + cells],
                own,
                (((1,), (1,)), ((), ())),
                preferred_element_type=jnp.float32,
            )
            partial[start : start + 3 * channels, :] = term * factor

    def input_terms(shift_x, first):
        for shift_y in (-1, 0, 1):
            tap = 9 * (shift_x + 1) + 3 * (shift_y + 1)
            term = jnp.dot(
                jnp.concatenate([weight_ref[tap + 2], weight_ref[tap + 1], weight_ref[tap]], axis=1),
                grad_rows[1 - shift_x, :, (1 - shift_y) * lanes : (1 - shift_y) * lanes + cells],
                preferred_element_type=jnp.float32,
            )
            if first and shift_y == -1:
                total[...] = term
            else:
                total[...] += term

    grad_plane(grad_ref[...], 0)
    hidden_plane(pre_ref[...], 0)
    weight_terms(0)
    arrive(0)
    hidden_plane(pre_halo[0], -1)
    hidden_plane(pre_halo[1], 1)
    weight_terms(-1)
    weight_terms(1)

    def finish_input():
        arrive(1)
        grad_plane(grad_halo[0], -1)
        grad_plane(grad_halo[1], 1)
        input_terms(-1, False)
        input_terms(1, False)
        for row in range(rows):
            plane[pl.ds(row, channels, stride=rows), :] = total[:, row * lanes : (row + 1) * lanes]
        back = plane[0 : channels * rows, :].reshape(channels, rows, lanes)
        act = pre_ref[...].astype(jnp.float32)
        grad_in_ref[...] = (back * jnp.where(act > 0, 1.0, slope)).astype(grad_in_ref.dtype)

    def own_input():
        weight_copy.wait()
        input_terms(0, True)

    if scatter:
        held, stages = stage_refs[0], stage_refs[1:]
        piece = partial.shape[0] // 8 * 8 - 8
        piece = piece // (space_count * batch_count)
        padded_piece = held.shape[-2]
        partial[partial.shape[0] - 8 :, :] = jnp.zeros((8, lanes), jnp.float32)
        for s in range(space_count):
            for b in range(batch_count):
                start = (s * batch_count + b) * piece
                held[b % 2, s // 2, b // 2, s % 2] = partial[start : start + padded_piece, :]
        waiting = []
        for number, axis in enumerate("cyzx"):
            received, summed, send_sem, recv_sem = stages[4 * number : 4 * number + 4]
            extent, mine = extents[axis], coords[axis]
            copies = []
            for step in range(1, extent):
                place = lax.rem(mine + step, extent)
                copy = pltpu.make_async_remote_copy(
                    src_ref=held.at[place],
                    dst_ref=received.at[step - 1],
                    send_sem=send_sem.at[step - 1],
                    recv_sem=recv_sem.at[step - 1],
                    device_id=peer(axis, place),
                    device_id_type=MESH,
                )
                copy.start()
                copies.append(copy)
            if axis == "c":
                own_input()
            if axis == "x":
                finish_input()
            value = held[mine]
            for step, copy in enumerate(copies):
                copy.wait_recv()
                value = value + received[step]
            waiting += copies
            if axis == "x":
                weight_grad_ref[...] = value
            else:
                summed[...] = value
                held = summed
        for copy in waiting:
            copy.wait_send()
    else:
        own_input()
        finish_input()
        weight_grad_ref[...] = partial[...]

    for index, (source, slots) in enumerate(pairs):
        for slot, condition in ((0, has_right), (1, has_left)):

            @pl.when(condition)
            def _():
                halo(source, slots, index, slot).wait_send()


def fused_device(pre_act, grad_out, weight):
    samples, channels, local_x, rows, lanes = pre_act.shape
    out_chan, taps = grad_out.shape[1], weight.shape[0]
    space_count, batch_count = lax.axis_size("space"), lax.axis_size("batch")
    fits = (
        samples == 1
        and local_x == 1
        and taps == 27
        and rows == 8
        and lanes == 128
        and out_chan == 128
        and channels % 16 == 0
        and space_count > 1
    )
    if not fits:
        return on_device(pre_act, grad_out, weight)
    count = samples * batch_count * local_x * space_count * rows * lanes
    factor = 1.0 / count**0.5
    devices = space_count * batch_count
    total_rows = taps * channels
    scatter = (
        space_count % 2 == 0 and batch_count % 2 == 0 and total_rows % devices == 0
    )
    cells = rows * lanes
    widest = max(channels, out_chan)
    bf16, f32 = jnp.bfloat16, jnp.float32
    scratch = [
        pltpu.VMEM((2, channels, rows, lanes), bf16),
        pltpu.VMEM((2, out_chan, rows, lanes), bf16),
        pltpu.VMEM((taps, channels, out_chan), bf16),
        pltpu.VMEM((widest * rows, lanes), f32),
        pltpu.VMEM((3, 3 * channels, cells + 2 * lanes), bf16),
        pltpu.VMEM((3, 3 * out_chan, cells + 2 * lanes), bf16),
        pltpu.VMEM((channels, cells), f32),
        pltpu.VMEM((total_rows + 8 if scatter else total_rows, out_chan), f32),
        pltpu.SemaphoreType.DMA((2, 2)),
        pltpu.SemaphoreType.DMA((2, 2)),
        pltpu.SemaphoreType.DMA,
    ]
    owned = total_rows
    if scatter:
        piece = total_rows // devices
        owned = -(-piece // 8) * 8
        sizes = [2, space_count // 2, batch_count // 2, 2]
        tile = (owned, out_chan)
        scratch.append(pltpu.VMEM((*sizes, *tile), f32))
        for number, extent in enumerate(sizes):
            rest = (*sizes[number + 1 :], *tile)
            scratch += [
                pltpu.VMEM((max(extent - 1, 1), *rest), f32),
                pltpu.VMEM(rest, f32),
                pltpu.SemaphoreType.DMA((max(extent - 1, 1),)),
                pltpu.SemaphoreType.DMA((max(extent - 1, 1),)),
            ]
    vmem = pl.BlockSpec(memory_space=pltpu.VMEM)
    grad_in, weight_grad = pl.pallas_call(
        functools.partial(kernel, (space_count, batch_count), factor, scatter),
        out_shape=(
            jax.ShapeDtypeStruct((channels, rows, lanes), bf16),
            jax.ShapeDtypeStruct((owned, out_chan), f32),
        ),
        in_specs=[vmem, vmem, pl.BlockSpec(memory_space=pl.ANY)],
        out_specs=(vmem, vmem),
        scratch_shapes=scratch,
        compiler_params=pltpu.CompilerParams(
            collective_id=0, has_side_effects=True, vmem_limit_bytes=48 * 2**20
        ),
    )(
        pre_act.reshape(channels, rows, lanes),
        grad_out.reshape(out_chan, rows, lanes),
        weight,
    )
    grad_in = grad_in.reshape(pre_act.shape)
    if scatter:
        return grad_in, weight_grad[:piece].reshape(-1)
    space_part = lax.psum_scatter(
        weight_grad.reshape(-1), "space", scatter_dimension=0, tiled=True
    )
    return grad_in, lax.psum_scatter(space_part, "batch", scatter_dimension=0, tiled=True)


def solution(mesh):
    return jax.shard_map(
        fused_device,
        mesh=mesh,
        in_specs=(
            P("batch", None, "space", None, None),
            P("batch", None, "space", None, None),
            P(),
        ),
        out_specs=(P("batch", None, "space", None, None), P(("space", "batch"))),
        check_vma=False,
    )
```

```python
import functools

import jax
import jax.numpy as jnp
from jax import lax
from jax.experimental import pallas as pl
from jax.experimental.pallas import tpu as pltpu
from jax.sharding import PartitionSpec as P

slope = 0.3


def padded(block, sides, width):
    for axis, dim in sides:
        count = lax.axis_size(axis)
        forward = [(i, i + 1) for i in range(count - 1)]
        backward = [(target, source) for source, target in forward]
        low = lax.ppermute(
            lax.slice_in_dim(block, block.shape[dim] - width, None, axis=dim), axis, forward
        )
        high = lax.ppermute(lax.slice_in_dim(block, 0, width, axis=dim), axis, backward)
        block = jnp.concatenate([low, block, high], axis=dim)
    return block


def leaky(values):
    return jnp.where(values > 0, values, slope * values)


def on_device(pre_act, grad_out, weight):
    local_x = pre_act.shape[2]
    local_y = pre_act.shape[3]
    local_z = pre_act.shape[4]
    count = (
        pre_act.shape[0]
        * lax.axis_size("batch")
        * local_x
        * lax.axis_size("space")
        * local_y
        * local_z
    )
    factor = 1.0 / jnp.sqrt(jnp.float32(count))
    act_float = pre_act.astype(jnp.float32)
    yz_pad = ((0, 0), (0, 0), (0, 0), (1, 1), (1, 1))
    grad_hidden = jnp.zeros(pre_act.shape, jnp.float32)
    tap_grads = []
    joined = jnp.concatenate([pre_act, grad_out], axis=1)
    widened = padded(joined, (("space", 2),), 1)
    in_chan = pre_act.shape[1]
    hidden_pad = jnp.pad(
        leaky(widened[:, :in_chan].astype(jnp.float32)).astype(jnp.bfloat16), yz_pad
    )
    grad_pad = jnp.pad(widened[:, in_chan:], yz_pad)
    for tap in range(27):
        shift_x = tap // 9 - 1
        shift_y = tap // 3 % 3 - 1
        shift_z = tap % 3 - 1
        window = grad_pad[
            :,
            :,
            1 - shift_x : 1 - shift_x + local_x,
            1 - shift_y : 1 - shift_y + local_y,
            1 - shift_z : 1 - shift_z + local_z,
        ]
        grad_hidden = grad_hidden + jnp.einsum(
            "ic,scxyz->sixyz", weight[tap], window, preferred_element_type=jnp.float32
        )
        moved = hidden_pad[
            :,
            :,
            1 + shift_x : 1 + shift_x + local_x,
            1 + shift_y : 1 + shift_y + local_y,
            1 + shift_z : 1 + shift_z + local_z,
        ]
        tap_grads.append(
            jnp.einsum("sixyz,scxyz->ic", moved, grad_out, preferred_element_type=jnp.float32)
        )
    grad_in = (grad_hidden * jnp.where(act_float > 0, 1.0, slope)).astype(jnp.bfloat16)
    partial_sum = (jnp.stack(tap_grads) * factor).reshape(-1)
    space_part = lax.psum_scatter(partial_sum, "space", scatter_dimension=0, tiled=True)
    weight_grad = lax.psum_scatter(space_part, "batch", scatter_dimension=0, tiled=True)
    return (grad_in, weight_grad)


MESH = pl.DeviceIdType.MESH


def prepare(values, scratch, target):
    channels, rows, lanes = values.shape
    scratch[0 : channels * rows, :] = values.reshape(channels * rows, lanes)
    lane = lax.broadcasted_iota(jnp.int32, (channels, lanes), 1)
    blank = jnp.zeros((3 * channels, lanes), target.dtype)
    target[:, 0:lanes] = blank
    target[:, (rows + 1) * lanes : (rows + 2) * lanes] = blank
    for row in range(rows):
        block = scratch[pl.ds(row, channels, stride=rows), :]
        before = jnp.where(lane == 0, 0.0, pltpu.roll(block, 1, 1))
        after = jnp.where(lane == lanes - 1, 0.0, pltpu.roll(block, lanes - 1, 1))
        for place, shifted in enumerate((before, block, after)):
            target[
                place * channels : (place + 1) * channels, (row + 1) * lanes : (row + 2) * lanes
            ] = shifted.astype(target.dtype)


def kernel(
    sizes,
    factor,
    scatter,
    pre_hbm,
    grad_hbm,
    weight_hbm,
    grad_in_ref,
    weight_grad_ref,
    pre_ref,
    grad_ref,
    weight_ref,
    pre_halo,
    grad_halo,
    plane,
    hidden_rows,
    grad_rows,
    total,
    partial,
    local_sem,
    direct_send,
    direct_recv,
    passed_send,
    passed_recv,
    *stage_refs,
):
    space_count, batch_count = sizes
    space, batch = lax.axis_index("space"), lax.axis_index("batch")
    channels, rows, lanes = pre_ref.shape
    out_chan = grad_ref.shape[0]
    cells = rows * lanes

    coords = dict(c=lax.rem(batch, 2), z=batch // 2, x=lax.rem(space, 2), y=space // 2)
    extents = dict(c=2, z=batch_count // 2, x=2, y=space_count // 2)
    side = coords["x"]

    def peer(axis, place):
        moved = dict(coords, **{axis: place})
        return (moved["y"] * 2 + moved["x"], moved["z"] * 2 + moved["c"])

    local = [
        pltpu.make_async_copy(source, target, local_sem.at[place])
        for place, (source, target) in enumerate(
            ((grad_hbm, grad_ref), (pre_hbm, pre_ref), (weight_hbm, weight_ref))
        )
    ]
    for copy in local:
        copy.start()

    barrier = pltpu.get_barrier_semaphore()
    low, high = space >= 2, space < space_count - 2
    if scatter:
        greeted = 0
        for axis, extent in extents.items():
            for step in range(1, extent):
                pl.semaphore_signal(
                    barrier,
                    inc=1,
                    device_id=peer(axis, lax.rem(coords[axis] + step, extent)),
                    device_id_type=MESH,
                )
                greeted += 1
        pl.semaphore_wait(barrier, greeted)
    else:
        pl.semaphore_signal(
            barrier, inc=1, device_id=peer("x", 1 - side), device_id_type=MESH
        )
        for there, condition in ((space - 2, low), (space + 2, high)):

            @pl.when(condition)
            def _():
                pl.semaphore_signal(barrier, inc=1, device_id=(there, batch), device_id_type=MESH)

        pl.semaphore_wait(barrier, 1 + jnp.where(low, 1, 0) + jnp.where(high, 1, 0))

    half = out_chan // 2
    messages = [
        (pre_hbm, lambda slot: pre_halo.at[slot]),
        (grad_hbm.at[0:half], lambda slot: grad_halo.at[slot, 0:half]),
        (grad_hbm.at[half:out_chan], lambda slot: grad_halo.at[slot, half:out_chan]),
    ]
    near = 1 - side
    passes = jnp.where(side == 0, space < space_count - 2, space >= 2)
    gets = jnp.where(side == 0, space >= 2, space < space_count - 2)
    beyond = jnp.where(side == 0, space + 2, space - 2)

    def direct(index):
        source, slots = messages[index]
        return pltpu.make_async_remote_copy(
            src_ref=source,
            dst_ref=slots(side),
            send_sem=direct_send.at[index],
            recv_sem=direct_recv.at[index],
            device_id=peer("x", 1 - side),
            device_id_type=MESH,
        )

    def passed(index):
        slots = messages[index][1]
        return pltpu.make_async_remote_copy(
            src_ref=slots(near),
            dst_ref=slots(side),
            send_sem=passed_send.at[index],
            recv_sem=passed_recv.at[index],
            device_id=(beyond, batch),
            device_id_type=MESH,
        )

    sent = [direct(index) for index in range(3)]
    for copy in sent:
        copy.start()

    def pass_on(index):
        sent[index].wait_recv()

        @pl.when(passes)
        def _():
            passed(index).start()

    def take(index, target):
        @pl.when(gets)
        def _():
            passed(index).wait_recv()

        @pl.when(jnp.logical_not(gets))
        def _():
            target[side] = jnp.zeros(target.shape[1:], target.dtype)

    def hidden_plane(values, place):
        prepare(leaky(values.astype(jnp.float32)), plane, hidden_rows.at[place])

    def grad_plane(values, place):
        prepare(values.astype(jnp.float32), plane, grad_rows.at[place])

    def weight_terms(place):
        own = grad_rows[1, out_chan : 2 * out_chan, lanes : lanes + cells]
        for shift_y in (-1, 0, 1):
            start = (9 * place + 3 * (shift_y + 1)) * channels
            if not isinstance(place, int):
                start = pl.multiple_of(start, 8)
            term = lax.dot_general(
                hidden_rows[place, :, (1 + shift_y) * lanes : (1 + shift_y) * lanes + cells],
                own,
                (((1,), (1,)), ((), ())),
                preferred_element_type=jnp.float32,
            )
            partial[pl.ds(start, 3 * channels), :] = term * factor

    def input_terms(place, first):
        for shift_y in (-1, 0, 1):
            tap = 9 * (2 - place) + 3 * (shift_y + 1)
            term = jnp.dot(
                jnp.concatenate([weight_ref[tap + 2], weight_ref[tap + 1], weight_ref[tap]], axis=1),
                grad_rows[place, :, (1 - shift_y) * lanes : (1 - shift_y) * lanes + cells],
                preferred_element_type=jnp.float32,
            )
            if first and shift_y == -1:
                total[...] = term
            else:
                total[...] += term

    near_place, far_place = 2 * near, 2 * side

    local[0].wait()
    local[1].wait()
    grad_plane(grad_ref[...], 1)
    hidden_plane(pre_ref[...], 1)
    pass_on(0)
    weight_terms(1)
    hidden_plane(pre_halo[near], near_place)
    weight_terms(near_place)
    local[2].wait()
    pass_on(1)
    take(0, pre_halo)
    hidden_plane(pre_halo[side], far_place)
    weight_terms(far_place)

    def near_input():
        grad_plane(grad_halo[near], near_place)
        input_terms(near_place, False)

    def far_input():
        @pl.when(gets)
        def _():
            passed(1).wait_recv()

        take(2, grad_halo)
        grad_plane(grad_halo[side], far_place)
        input_terms(far_place, False)
        for row in range(rows):
            plane[pl.ds(row, channels, stride=rows), :] = total[:, row * lanes : (row + 1) * lanes]
        back = plane[0 : channels * rows, :].reshape(channels, rows, lanes)
        act = pre_ref[...].astype(jnp.float32)
        grad_in_ref[...] = (back * jnp.where(act > 0, 1.0, slope)).astype(grad_in_ref.dtype)

    waiting = list(sent)
    if scatter:
        held, stages = stage_refs[0], stage_refs[1:]
        padded_piece = held.shape[-2]
        piece = (partial.shape[0] - 8) // (space_count * batch_count)
        partial[partial.shape[0] - 8 :, :] = jnp.zeros((8, lanes), jnp.float32)

        def pack(chunk):
            for y in range(extents["y"]):
                for b in range(batch_count):
                    start = ((2 * y + chunk) * batch_count + b) * piece
                    held[b % 2, chunk, y, b // 2] = partial[start : start + padded_piece, :]

        def refs(axis):
            number = "cyzx".index(axis)
            return stages[4 * number : 4 * number + 4]

        def begin(axis, chunk):
            received, _, send_sem, recv_sem = refs(axis)
            copies = []
            for step in range(1, extents[axis]):
                place = lax.rem(coords[axis] + step, extents[axis])
                if axis == "c":
                    source = held.at[place, chunk]
                else:
                    source = refs("cyz"["cyz".index(axis) - 1])[1].at[chunk, place]
                copy = pltpu.make_async_remote_copy(
                    src_ref=source,
                    dst_ref=received.at[chunk, step - 1],
                    send_sem=send_sem.at[chunk, step - 1],
                    recv_sem=recv_sem.at[chunk, step - 1],
                    device_id=peer(axis, place),
                    device_id_type=MESH,
                )
                copy.start()
                copies.append(copy)
            waiting.extend(copies)
            return copies

        def end(axis, chunk, copies):
            received, summed = refs(axis)[:2]
            mine = coords[axis]
            if axis == "c":
                value = held[mine, chunk]
            else:
                value = refs("cyz"["cyz".index(axis) - 1])[1][chunk, mine]
            for step, copy in enumerate(copies):
                copy.wait_recv()
                value = value + received[chunk, step]
            summed[chunk] = value

        flights = {}
        for chunk in range(2):
            pack(chunk)
            flights["c", chunk] = begin("c", chunk)
        pass_on(2)
        input_terms(1, True)
        for chunk in range(2):
            end("c", chunk, flights["c", chunk])
            flights["y", chunk] = begin("y", chunk)
        near_input()
        for chunk in range(2):
            end("y", chunk, flights["y", chunk])
            flights["z", chunk] = begin("z", chunk)
        far_input()
        for chunk in range(2):
            end("z", chunk, flights["z", chunk])
        received, _, send_sem, recv_sem = refs("x")
        kept = refs("z")[1]
        copy = pltpu.make_async_remote_copy(
            src_ref=kept.at[1 - side],
            dst_ref=received,
            send_sem=send_sem,
            recv_sem=recv_sem,
            device_id=peer("x", 1 - side),
            device_id_type=MESH,
        )
        copy.start()
        waiting.append(copy)
        copy.wait_recv()
        weight_grad_ref[...] = kept[side] + received[...]
    else:
        pass_on(2)
        input_terms(1, True)
        near_input()
        far_input()
        weight_grad_ref[...] = partial[...]

    for copy in waiting:
        copy.wait_send()

    @pl.when(passes)
    def _():
        for index in range(3):
            passed(index).wait_send()


def fused_device(pre_act, grad_out, weight):
    samples, channels, local_x, rows, lanes = pre_act.shape
    out_chan, taps = grad_out.shape[1], weight.shape[0]
    space_count, batch_count = lax.axis_size("space"), lax.axis_size("batch")
    fits = (
        samples == 1
        and local_x == 1
        and taps == 27
        and rows == 8
        and lanes == 128
        and out_chan == 128
        and channels % 16 == 0
        and space_count % 2 == 0
    )
    if not fits:
        return on_device(pre_act, grad_out, weight)
    count = samples * batch_count * local_x * space_count * rows * lanes
    factor = 1.0 / count**0.5
    devices = space_count * batch_count
    total_rows = taps * channels
    scatter = (
        space_count > 2 and batch_count % 2 == 0 and batch_count > 2 and total_rows % devices == 0
    )
    cells = rows * lanes
    widest = max(channels, out_chan)
    bf16, f32 = jnp.bfloat16, jnp.float32
    scratch = [
        pltpu.VMEM((channels, rows, lanes), bf16),
        pltpu.VMEM((out_chan, rows, lanes), bf16),
        pltpu.VMEM((taps, channels, out_chan), bf16),
        pltpu.VMEM((2, channels, rows, lanes), bf16),
        pltpu.VMEM((2, out_chan, rows, lanes), bf16),
        pltpu.VMEM((widest * rows, lanes), f32),
        pltpu.VMEM((3, 3 * channels, cells + 2 * lanes), bf16),
        pltpu.VMEM((3, 3 * out_chan, cells + 2 * lanes), bf16),
        pltpu.VMEM((channels, cells), f32),
        pltpu.VMEM((total_rows + 8 if scatter else total_rows, out_chan), f32),
        *[pltpu.SemaphoreType.DMA((3,))] * 5,
    ]
    owned = total_rows
    if scatter:
        piece = total_rows // devices
        owned = -(-piece // 8) * 8
        sizes = [space_count // 2, batch_count // 2]
        tile = (owned, out_chan)
        scratch.append(pltpu.VMEM((2, 2, *sizes, *tile), f32))
        for number, extent in enumerate([2, *sizes]):
            rest = (*sizes[number:], *tile)
            scratch += [
                pltpu.VMEM((2, extent - 1, *rest), f32),
                pltpu.VMEM((2, *rest), f32),
                pltpu.SemaphoreType.DMA((2, extent - 1)),
                pltpu.SemaphoreType.DMA((2, extent - 1)),
            ]
        scratch += [
            pltpu.VMEM(tile, f32),
            pltpu.VMEM(tile, f32),
            pltpu.SemaphoreType.DMA,
            pltpu.SemaphoreType.DMA,
        ]
    vmem = pl.BlockSpec(memory_space=pltpu.VMEM)
    grad_in, weight_grad = pl.pallas_call(
        functools.partial(kernel, (space_count, batch_count), factor, scatter),
        out_shape=(
            jax.ShapeDtypeStruct((channels, rows, lanes), bf16),
            jax.ShapeDtypeStruct((owned, out_chan), f32),
        ),
        in_specs=[pl.BlockSpec(memory_space=pltpu.HBM)] * 3,
        out_specs=(vmem, vmem),
        scratch_shapes=scratch,
        compiler_params=pltpu.CompilerParams(
            collective_id=0, has_side_effects=True, vmem_limit_bytes=67043328
        ),
    )(
        pre_act.reshape(channels, rows, lanes),
        grad_out.reshape(out_chan, rows, lanes),
        weight,
    )
    grad_in = grad_in.reshape(pre_act.shape)
    if scatter:
        return grad_in, weight_grad[:piece].reshape(-1)
    space_part = lax.psum_scatter(
        weight_grad.reshape(-1), "space", scatter_dimension=0, tiled=True
    )
    return grad_in, lax.psum_scatter(space_part, "batch", scatter_dimension=0, tiled=True)


def solution(mesh):
    return jax.shard_map(
        fused_device,
        mesh=mesh,
        in_specs=(
            P("batch", None, "space", None, None),
            P("batch", None, "space", None, None),
            P(),
        ),
        out_specs=(P("batch", None, "space", None, None), P(("space", "batch"))),
        check_vma=False,
    )
```

```python
import functools

import jax
import jax.numpy as jnp
from jax import lax
from jax.experimental import pallas as pl
from jax.experimental.pallas import tpu as pltpu
from jax.sharding import PartitionSpec as P

slope = 0.3


def padded(block, sides, width):
    for axis, dim in sides:
        count = lax.axis_size(axis)
        forward = [(i, i + 1) for i in range(count - 1)]
        backward = [(target, source) for source, target in forward]
        low = lax.ppermute(
            lax.slice_in_dim(block, block.shape[dim] - width, None, axis=dim), axis, forward
        )
        high = lax.ppermute(lax.slice_in_dim(block, 0, width, axis=dim), axis, backward)
        block = jnp.concatenate([low, block, high], axis=dim)
    return block


def leaky(values):
    return jnp.where(values > 0, values, slope * values)


def on_device(pre_act, grad_out, weight):
    local_x = pre_act.shape[2]
    local_y = pre_act.shape[3]
    local_z = pre_act.shape[4]
    count = (
        pre_act.shape[0]
        * lax.axis_size("batch")
        * local_x
        * lax.axis_size("space")
        * local_y
        * local_z
    )
    factor = 1.0 / jnp.sqrt(jnp.float32(count))
    act_float = pre_act.astype(jnp.float32)
    yz_pad = ((0, 0), (0, 0), (0, 0), (1, 1), (1, 1))
    grad_hidden = jnp.zeros(pre_act.shape, jnp.float32)
    tap_grads = []
    joined = jnp.concatenate([pre_act, grad_out], axis=1)
    widened = padded(joined, (("space", 2),), 1)
    in_chan = pre_act.shape[1]
    hidden_pad = jnp.pad(
        leaky(widened[:, :in_chan].astype(jnp.float32)).astype(jnp.bfloat16), yz_pad
    )
    grad_pad = jnp.pad(widened[:, in_chan:], yz_pad)
    for tap in range(27):
        shift_x = tap // 9 - 1
        shift_y = tap // 3 % 3 - 1
        shift_z = tap % 3 - 1
        window = grad_pad[
            :,
            :,
            1 - shift_x : 1 - shift_x + local_x,
            1 - shift_y : 1 - shift_y + local_y,
            1 - shift_z : 1 - shift_z + local_z,
        ]
        grad_hidden = grad_hidden + jnp.einsum(
            "ic,scxyz->sixyz", weight[tap], window, preferred_element_type=jnp.float32
        )
        moved = hidden_pad[
            :,
            :,
            1 + shift_x : 1 + shift_x + local_x,
            1 + shift_y : 1 + shift_y + local_y,
            1 + shift_z : 1 + shift_z + local_z,
        ]
        tap_grads.append(
            jnp.einsum("sixyz,scxyz->ic", moved, grad_out, preferred_element_type=jnp.float32)
        )
    grad_in = (grad_hidden * jnp.where(act_float > 0, 1.0, slope)).astype(jnp.bfloat16)
    partial_sum = (jnp.stack(tap_grads) * factor).reshape(-1)
    space_part = lax.psum_scatter(partial_sum, "space", scatter_dimension=0, tiled=True)
    weight_grad = lax.psum_scatter(space_part, "batch", scatter_dimension=0, tiled=True)
    return (grad_in, weight_grad)


MESH = pl.DeviceIdType.MESH


def prepare(values, scratch, target):
    channels, rows, lanes = values.shape
    scratch[0 : channels * rows, :] = values.reshape(channels * rows, lanes)
    lane = lax.broadcasted_iota(jnp.int32, (channels, lanes), 1)
    blank = jnp.zeros((3 * channels, lanes), target.dtype)
    target[:, 0:lanes] = blank
    target[:, (rows + 1) * lanes : (rows + 2) * lanes] = blank
    for row in range(rows):
        block = scratch[pl.ds(row, channels, stride=rows), :]
        before = jnp.where(lane == 0, 0.0, pltpu.roll(block, 1, 1))
        after = jnp.where(lane == lanes - 1, 0.0, pltpu.roll(block, lanes - 1, 1))
        for place, shifted in enumerate((before, block, after)):
            target[
                place * channels : (place + 1) * channels, (row + 1) * lanes : (row + 2) * lanes
            ] = shifted.astype(target.dtype)


def kernel(
    sizes,
    factor,
    scatter,
    pre_hbm,
    grad_hbm,
    weight_hbm,
    grad_in_ref,
    weight_grad_ref,
    pre_ref,
    grad_ref,
    weight_ref,
    pre_halo,
    grad_halo,
    plane,
    hidden_rows,
    grad_rows,
    total,
    partial,
    local_sem,
    direct_send,
    direct_recv,
    passed_send,
    passed_recv,
    *stage_refs,
):
    space_count, batch_count = sizes
    space, batch = lax.axis_index("space"), lax.axis_index("batch")
    channels, rows, lanes = pre_ref.shape
    out_chan = grad_ref.shape[0]
    cells = rows * lanes

    coords = dict(c=lax.rem(batch, 2), z=batch // 2, x=lax.rem(space, 2), y=space // 2)
    extents = dict(c=2, z=batch_count // 2, x=2, y=space_count // 2)
    side = coords["x"]

    def peer(axis, place):
        moved = dict(coords, **{axis: place})
        return (moved["y"] * 2 + moved["x"], moved["z"] * 2 + moved["c"])

    local = [
        pltpu.make_async_copy(source, target, local_sem.at[place])
        for place, (source, target) in enumerate(
            ((grad_hbm, grad_ref), (pre_hbm, pre_ref), (weight_hbm, weight_ref))
        )
    ]
    for copy in local:
        copy.start()

    barrier = pltpu.get_barrier_semaphore()
    low, high = space >= 2, space < space_count - 2
    if scatter:
        greeted = 0
        for axis, extent in extents.items():
            for step in range(1, extent):
                pl.semaphore_signal(
                    barrier,
                    inc=1,
                    device_id=peer(axis, lax.rem(coords[axis] + step, extent)),
                    device_id_type=MESH,
                )
                greeted += 1
        pl.semaphore_wait(barrier, greeted)
    else:
        pl.semaphore_signal(
            barrier, inc=1, device_id=peer("x", 1 - side), device_id_type=MESH
        )
        for there, condition in ((space - 2, low), (space + 2, high)):

            @pl.when(condition)
            def _():
                pl.semaphore_signal(barrier, inc=1, device_id=(there, batch), device_id_type=MESH)

        pl.semaphore_wait(barrier, 1 + jnp.where(low, 1, 0) + jnp.where(high, 1, 0))

    half = out_chan // 2
    messages = [
        (pre_hbm, lambda slot: pre_halo.at[slot]),
        (grad_hbm.at[0:half], lambda slot: grad_halo.at[slot, 0:half]),
        (grad_hbm.at[half:out_chan], lambda slot: grad_halo.at[slot, half:out_chan]),
    ]
    near = 1 - side
    passes = jnp.where(side == 0, space < space_count - 2, space >= 2)
    gets = jnp.where(side == 0, space >= 2, space < space_count - 2)
    beyond = jnp.where(side == 0, space + 2, space - 2)

    def direct(index):
        source, slots = messages[index]
        return pltpu.make_async_remote_copy(
            src_ref=source,
            dst_ref=slots(side),
            send_sem=direct_send.at[index],
            recv_sem=direct_recv.at[index],
            device_id=peer("x", 1 - side),
            device_id_type=MESH,
        )

    def passed(index):
        slots = messages[index][1]
        return pltpu.make_async_remote_copy(
            src_ref=slots(near),
            dst_ref=slots(side),
            send_sem=passed_send.at[index],
            recv_sem=passed_recv.at[index],
            device_id=(beyond, batch),
            device_id_type=MESH,
        )

    sent = [direct(index) for index in range(3)]
    for copy in sent:
        copy.start()

    def pass_on(index):
        sent[index].wait_recv()

        @pl.when(passes)
        def _():
            passed(index).start()

    def take(index, target):
        @pl.when(gets)
        def _():
            passed(index).wait_recv()

        @pl.when(jnp.logical_not(gets))
        def _():
            target[side] = jnp.zeros(target.shape[1:], target.dtype)

    def hidden_plane(values, place):
        prepare(leaky(values.astype(jnp.float32)), plane, hidden_rows.at[place])

    def grad_plane(values, place):
        prepare(values.astype(jnp.float32), plane, grad_rows.at[place])

    def weight_terms(place):
        own = grad_rows[1, out_chan : 2 * out_chan, lanes : lanes + cells]
        for shift_y in (-1, 0, 1):
            start = (9 * place + 3 * (shift_y + 1)) * channels
            if not isinstance(place, int):
                start = pl.multiple_of(start, 8)
            term = lax.dot_general(
                hidden_rows[place, :, (1 + shift_y) * lanes : (1 + shift_y) * lanes + cells],
                own,
                (((1,), (1,)), ((), ())),
                preferred_element_type=jnp.float32,
            )
            partial[pl.ds(start, 3 * channels), :] = term * factor

    def input_terms(place, first):
        for shift_y in (-1, 0, 1):
            tap = 9 * (2 - place) + 3 * (shift_y + 1)
            term = jnp.dot(
                jnp.concatenate([weight_ref[tap + 2], weight_ref[tap + 1], weight_ref[tap]], axis=1),
                grad_rows[place, :, (1 - shift_y) * lanes : (1 - shift_y) * lanes + cells],
                preferred_element_type=jnp.float32,
            )
            if first and shift_y == -1:
                total[...] = term
            else:
                total[...] += term

    near_place, far_place = 2 * near, 2 * side

    local[0].wait()
    local[1].wait()
    grad_plane(grad_ref[...], 1)
    hidden_plane(pre_ref[...], 1)
    pass_on(0)
    weight_terms(1)
    hidden_plane(pre_halo[near], near_place)
    weight_terms(near_place)
    local[2].wait()
    pass_on(1)
    take(0, pre_halo)
    hidden_plane(pre_halo[side], far_place)
    weight_terms(far_place)

    def near_input():
        grad_plane(grad_halo[near], near_place)
        input_terms(near_place, False)

    def far_input():
        @pl.when(gets)
        def _():
            passed(1).wait_recv()

        take(2, grad_halo)
        grad_plane(grad_halo[side], far_place)
        input_terms(far_place, False)
        for row in range(rows):
            plane[pl.ds(row, channels, stride=rows), :] = total[:, row * lanes : (row + 1) * lanes]
        back = plane[0 : channels * rows, :].reshape(channels, rows, lanes)
        act = pre_ref[...].astype(jnp.float32)
        grad_in_ref[...] = (back * jnp.where(act > 0, 1.0, slope)).astype(grad_in_ref.dtype)

    waiting = list(sent)
    if scatter:
        piece = (partial.shape[0] - 8) // (space_count * batch_count)
        partial[partial.shape[0] - 8 :, :] = jnp.zeros((8, lanes), jnp.float32)
        per_chunk = len(stage_refs) // 2
        chunks, first_row = [], 0
        for number, order in enumerate(("cxyz", "cyxz")):
            refs = stage_refs[number * per_chunk : (number + 1) * per_chunk]
            chunks.append((order, refs[0], refs[1:], first_row, refs[0].shape[-2]))
            first_row += refs[0].shape[-2]

        def pack(order, held, first_row, count):
            for s in range(space_count):
                for b in range(batch_count):
                    start = (s * batch_count + b) * piece + first_row
                    place = dict(c=b % 2, z=b // 2, x=s % 2, y=s // 2)
                    index = tuple(place[axis] for axis in order)
                    held[index] = partial[start : start + count, :]

        def source_of(chunk, number):
            return chunk[1] if number == 0 else chunk[2][4 * number - 3]

        def begin(chunk, number):
            axis = chunk[0][number]
            received, _, send_sem, recv_sem = chunk[2][4 * number : 4 * number + 4]
            copies = []
            for step in range(1, extents[axis]):
                place = lax.rem(coords[axis] + step, extents[axis])
                copy = pltpu.make_async_remote_copy(
                    src_ref=source_of(chunk, number).at[place],
                    dst_ref=received.at[step - 1],
                    send_sem=send_sem.at[step - 1],
                    recv_sem=recv_sem.at[step - 1],
                    device_id=peer(axis, place),
                    device_id_type=MESH,
                )
                copy.start()
                copies.append(copy)
            waiting.extend(copies)
            return copies

        def end(chunk, number, copies):
            received, summed = chunk[2][4 * number : 4 * number + 2]
            value = source_of(chunk, number)[coords[chunk[0][number]]]
            for step, copy in enumerate(copies):
                copy.wait_recv()
                value = value + received[step]
            if number < 3:
                summed[...] = value
            else:
                weight_grad_ref[chunk[3] : chunk[3] + chunk[4], :] = value

        flights = []
        for chunk in chunks:
            pack(chunk[0], chunk[1], chunk[3], chunk[4])
            flights.append(begin(chunk, 0))
        pass_on(2)
        for number in range(1, 4):
            for place, chunk in enumerate(chunks):
                end(chunk, number - 1, flights[place])
                flights[place] = begin(chunk, number)
            if number == 1:
                input_terms(1, True)
            elif number == 2:
                near_input()
            else:
                far_input()
        for place, chunk in enumerate(chunks):
            end(chunk, 3, flights[place])
    else:
        pass_on(2)
        input_terms(1, True)
        near_input()
        far_input()
        weight_grad_ref[...] = partial[...]

    for copy in waiting:
        copy.wait_send()

    @pl.when(passes)
    def _():
        for index in range(3):
            passed(index).wait_send()


def fused_device(pre_act, grad_out, weight):
    samples, channels, local_x, rows, lanes = pre_act.shape
    out_chan, taps = grad_out.shape[1], weight.shape[0]
    space_count, batch_count = lax.axis_size("space"), lax.axis_size("batch")
    fits = (
        samples == 1
        and local_x == 1
        and taps == 27
        and rows == 8
        and lanes == 128
        and out_chan == 128
        and channels % 16 == 0
        and space_count % 2 == 0
    )
    if not fits:
        return on_device(pre_act, grad_out, weight)
    count = samples * batch_count * local_x * space_count * rows * lanes
    factor = 1.0 / count**0.5
    devices = space_count * batch_count
    total_rows = taps * channels
    scatter = (
        space_count > 2 and batch_count % 2 == 0 and batch_count > 2 and total_rows % devices == 0
        and total_rows // devices > 8
    )
    cells = rows * lanes
    widest = max(channels, out_chan)
    bf16, f32 = jnp.bfloat16, jnp.float32
    scratch = [
        pltpu.VMEM((channels, rows, lanes), bf16),
        pltpu.VMEM((out_chan, rows, lanes), bf16),
        pltpu.VMEM((taps, channels, out_chan), bf16),
        pltpu.VMEM((2, channels, rows, lanes), bf16),
        pltpu.VMEM((2, out_chan, rows, lanes), bf16),
        pltpu.VMEM((widest * rows, lanes), f32),
        pltpu.VMEM((3, 3 * channels, cells + 2 * lanes), bf16),
        pltpu.VMEM((3, 3 * out_chan, cells + 2 * lanes), bf16),
        pltpu.VMEM((channels, cells), f32),
        pltpu.VMEM((total_rows + 8 if scatter else total_rows, out_chan), f32),
        *[pltpu.SemaphoreType.DMA((3,))] * 5,
    ]
    owned = total_rows
    if scatter:
        piece = total_rows // devices
        owned = -(-piece // 8) * 8
        extents = dict(c=2, x=2, y=space_count // 2, z=batch_count // 2)
        upper = -(-owned // 16) * 8
        for order, count in (("cxyz", upper), ("cyxz", owned - upper)):
            sizes = [extents[axis] for axis in order]
            scratch.append(pltpu.VMEM((*sizes, count, out_chan), f32))
            for number, extent in enumerate(sizes):
                rest = (*sizes[number + 1 :], count, out_chan)
                scratch += [
                    pltpu.VMEM((extent - 1, *rest), f32),
                    pltpu.VMEM(rest, f32),
                    pltpu.SemaphoreType.DMA((extent - 1,)),
                    pltpu.SemaphoreType.DMA((extent - 1,)),
                ]
    vmem = pl.BlockSpec(memory_space=pltpu.VMEM)
    grad_in, weight_grad = pl.pallas_call(
        functools.partial(kernel, (space_count, batch_count), factor, scatter),
        out_shape=(
            jax.ShapeDtypeStruct((channels, rows, lanes), bf16),
            jax.ShapeDtypeStruct((owned, out_chan), f32),
        ),
        in_specs=[pl.BlockSpec(memory_space=pltpu.HBM)] * 3,
        out_specs=(vmem, vmem),
        scratch_shapes=scratch,
        compiler_params=pltpu.CompilerParams(
            collective_id=0, has_side_effects=True, vmem_limit_bytes=48 * 2**20
        ),
    )(
        pltpu.with_memory_space_constraint(pre_act.reshape(channels, rows, lanes), pltpu.HBM),
        pltpu.with_memory_space_constraint(grad_out.reshape(out_chan, rows, lanes), pltpu.HBM),
        pltpu.with_memory_space_constraint(weight, pltpu.HBM),
    )
    grad_in = grad_in.reshape(pre_act.shape)
    if scatter:
        return grad_in, weight_grad[:piece].reshape(-1)
    space_part = lax.psum_scatter(
        weight_grad.reshape(-1), "space", scatter_dimension=0, tiled=True
    )
    return grad_in, lax.psum_scatter(space_part, "batch", scatter_dimension=0, tiled=True)


def solution(mesh):
    return jax.shard_map(
        fused_device,
        mesh=mesh,
        in_specs=(
            P("batch", None, "space", None, None),
            P("batch", None, "space", None, None),
            P(),
        ),
        out_specs=(P("batch", None, "space", None, None), P(("space", "batch"))),
        check_vma=False,
    )
```

```python
import functools

import jax
import jax.numpy as jnp
from jax import lax
from jax.experimental import pallas as pl
from jax.experimental.pallas import tpu as pltpu
from jax.sharding import PartitionSpec as P

slope = 0.3


def padded(block, sides, width):
    for axis, dim in sides:
        count = lax.axis_size(axis)
        forward = [(i, i + 1) for i in range(count - 1)]
        backward = [(target, source) for source, target in forward]
        low = lax.ppermute(
            lax.slice_in_dim(block, block.shape[dim] - width, None, axis=dim), axis, forward
        )
        high = lax.ppermute(lax.slice_in_dim(block, 0, width, axis=dim), axis, backward)
        block = jnp.concatenate([low, block, high], axis=dim)
    return block


def leaky(values):
    return jnp.where(values > 0, values, slope * values)


def on_device(pre_act, grad_out, weight):
    local_x = pre_act.shape[2]
    local_y = pre_act.shape[3]
    local_z = pre_act.shape[4]
    count = (
        pre_act.shape[0]
        * lax.axis_size("batch")
        * local_x
        * lax.axis_size("space")
        * local_y
        * local_z
    )
    factor = 1.0 / jnp.sqrt(jnp.float32(count))
    act_float = pre_act.astype(jnp.float32)
    yz_pad = ((0, 0), (0, 0), (0, 0), (1, 1), (1, 1))
    grad_hidden = jnp.zeros(pre_act.shape, jnp.float32)
    tap_grads = []
    joined = jnp.concatenate([pre_act, grad_out], axis=1)
    widened = padded(joined, (("space", 2),), 1)
    in_chan = pre_act.shape[1]
    hidden_pad = jnp.pad(
        leaky(widened[:, :in_chan].astype(jnp.float32)).astype(jnp.bfloat16), yz_pad
    )
    grad_pad = jnp.pad(widened[:, in_chan:], yz_pad)
    for tap in range(27):
        shift_x = tap // 9 - 1
        shift_y = tap // 3 % 3 - 1
        shift_z = tap % 3 - 1
        window = grad_pad[
            :,
            :,
            1 - shift_x : 1 - shift_x + local_x,
            1 - shift_y : 1 - shift_y + local_y,
            1 - shift_z : 1 - shift_z + local_z,
        ]
        grad_hidden = grad_hidden + jnp.einsum(
            "ic,scxyz->sixyz", weight[tap], window, preferred_element_type=jnp.float32
        )
        moved = hidden_pad[
            :,
            :,
            1 + shift_x : 1 + shift_x + local_x,
            1 + shift_y : 1 + shift_y + local_y,
            1 + shift_z : 1 + shift_z + local_z,
        ]
        tap_grads.append(
            jnp.einsum("sixyz,scxyz->ic", moved, grad_out, preferred_element_type=jnp.float32)
        )
    grad_in = (grad_hidden * jnp.where(act_float > 0, 1.0, slope)).astype(jnp.bfloat16)
    partial_sum = (jnp.stack(tap_grads) * factor).reshape(-1)
    space_part = lax.psum_scatter(partial_sum, "space", scatter_dimension=0, tiled=True)
    weight_grad = lax.psum_scatter(space_part, "batch", scatter_dimension=0, tiled=True)
    return (grad_in, weight_grad)


MESH = pl.DeviceIdType.MESH


def prepare(values, scratch, target):
    channels, rows, lanes = values.shape
    scratch[0 : channels * rows, :] = values.reshape(channels * rows, lanes)
    lane = lax.broadcasted_iota(jnp.int32, (channels, lanes), 1)
    blank = jnp.zeros((3 * channels, lanes), target.dtype)
    target[:, 0:lanes] = blank
    target[:, (rows + 1) * lanes : (rows + 2) * lanes] = blank
    for row in range(rows):
        block = scratch[pl.ds(row, channels, stride=rows), :]
        before = jnp.where(lane == 0, 0.0, pltpu.roll(block, 1, 1))
        after = jnp.where(lane == lanes - 1, 0.0, pltpu.roll(block, lanes - 1, 1))
        for place, shifted in enumerate((before, block, after)):
            target[
                place * channels : (place + 1) * channels, (row + 1) * lanes : (row + 2) * lanes
            ] = shifted.astype(target.dtype)


def kernel(
    sizes,
    factor,
    orders,
    pre_hbm,
    grad_hbm,
    weight_hbm,
    grad_in_ref,
    weight_grad_ref,
    pre_ref,
    grad_ref,
    weight_ref,
    pre_halo,
    grad_halo,
    plane,
    hidden_rows,
    grad_rows,
    total,
    partial,
    local_sem,
    direct_send,
    direct_recv,
    passed_send,
    passed_recv,
    *stage_refs,
):
    space_count, batch_count = sizes
    space, batch = lax.axis_index("space"), lax.axis_index("batch")
    channels, rows, lanes = pre_ref.shape
    out_chan = grad_ref.shape[0]
    cells = rows * lanes

    coords = dict(c=lax.rem(batch, 2), z=batch // 2, x=lax.rem(space, 2), y=space // 2)
    extents = dict(c=2, z=batch_count // 2, x=2, y=space_count // 2)
    side = coords["x"]

    def peer(axis, place):
        moved = dict(coords, **{axis: place})
        return (moved["y"] * 2 + moved["x"], moved["z"] * 2 + moved["c"])

    local = [
        pltpu.make_async_copy(source, target, local_sem.at[place])
        for place, (source, target) in enumerate(
            ((grad_hbm, grad_ref), (pre_hbm, pre_ref), (weight_hbm, weight_ref))
        )
    ]
    for copy in local:
        copy.start()

    barrier = pltpu.get_barrier_semaphore()
    low, high = space >= 2, space < space_count - 2
    if orders:
        greeted = 0
        for axis, extent in extents.items():
            for step in range(1, extent):
                pl.semaphore_signal(
                    barrier,
                    inc=1,
                    device_id=peer(axis, lax.rem(coords[axis] + step, extent)),
                    device_id_type=MESH,
                )
                greeted += 1
        pl.semaphore_wait(barrier, greeted)
    else:
        pl.semaphore_signal(
            barrier, inc=1, device_id=peer("x", 1 - side), device_id_type=MESH
        )
        for there, condition in ((space - 2, low), (space + 2, high)):

            @pl.when(condition)
            def _():
                pl.semaphore_signal(barrier, inc=1, device_id=(there, batch), device_id_type=MESH)

        pl.semaphore_wait(barrier, 1 + jnp.where(low, 1, 0) + jnp.where(high, 1, 0))

    half, quarter = out_chan // 2, channels // 2
    messages = [
        (pre_hbm.at[0:quarter], lambda slot: pre_halo.at[slot, 0:quarter]),
        (pre_hbm.at[quarter:channels], lambda slot: pre_halo.at[slot, quarter:channels]),
        (grad_hbm.at[0:half], lambda slot: grad_halo.at[slot, 0:half]),
        (grad_hbm.at[half:out_chan], lambda slot: grad_halo.at[slot, half:out_chan]),
    ]
    near = 1 - side
    passes = jnp.where(side == 0, space < space_count - 2, space >= 2)
    gets = jnp.where(side == 0, space >= 2, space < space_count - 2)
    beyond = jnp.where(side == 0, space + 2, space - 2)

    def direct(index):
        source, slots = messages[index]
        return pltpu.make_async_remote_copy(
            src_ref=source,
            dst_ref=slots(side),
            send_sem=direct_send.at[index],
            recv_sem=direct_recv.at[index],
            device_id=peer("x", 1 - side),
            device_id_type=MESH,
        )

    def passed(index):
        slots = messages[index][1]
        return pltpu.make_async_remote_copy(
            src_ref=slots(near),
            dst_ref=slots(side),
            send_sem=passed_send.at[index],
            recv_sem=passed_recv.at[index],
            device_id=(beyond, batch),
            device_id_type=MESH,
        )

    sent = [direct(index) for index in range(4)]
    for copy in sent:
        copy.start()

    def pass_on(index):
        sent[index].wait_recv()

        @pl.when(passes)
        def _():
            passed(index).start()

    def take(first, target):
        @pl.when(gets)
        def _():
            passed(first).wait_recv()
            passed(first + 1).wait_recv()

        @pl.when(jnp.logical_not(gets))
        def _():
            target[side] = jnp.zeros(target.shape[1:], target.dtype)

    def hidden_plane(values, place):
        prepare(leaky(values.astype(jnp.float32)), plane, hidden_rows.at[place])

    def grad_plane(values, place):
        prepare(values.astype(jnp.float32), plane, grad_rows.at[place])

    def weight_terms(place):
        own = grad_rows[1, out_chan : 2 * out_chan, lanes : lanes + cells]
        for shift_y in (-1, 0, 1):
            start = (9 * place + 3 * (shift_y + 1)) * channels
            if not isinstance(place, int):
                start = pl.multiple_of(start, 8)
            term = lax.dot_general(
                hidden_rows[place, :, (1 + shift_y) * lanes : (1 + shift_y) * lanes + cells],
                own,
                (((1,), (1,)), ((), ())),
                preferred_element_type=jnp.float32,
            )
            partial[pl.ds(start, 3 * channels), :] = term * factor

    def input_terms(place, first):
        for shift_y in (-1, 0, 1):
            tap = 9 * (2 - place) + 3 * (shift_y + 1)
            term = jnp.dot(
                jnp.concatenate([weight_ref[tap + 2], weight_ref[tap + 1], weight_ref[tap]], axis=1),
                grad_rows[place, :, (1 - shift_y) * lanes : (1 - shift_y) * lanes + cells],
                preferred_element_type=jnp.float32,
            )
            if first and shift_y == -1:
                total[...] = term
            else:
                total[...] += term

    near_place, far_place = 2 * near, 2 * side

    local[0].wait()
    local[1].wait()
    grad_plane(grad_ref[...], 1)
    hidden_plane(pre_ref[...], 1)
    pass_on(0)
    pass_on(1)
    weight_terms(1)
    hidden_plane(pre_halo[near], near_place)
    weight_terms(near_place)
    local[2].wait()
    take(0, pre_halo)
    hidden_plane(pre_halo[side], far_place)
    weight_terms(far_place)

    def near_input():
        grad_plane(grad_halo[near], near_place)
        input_terms(near_place, False)

    def far_input():
        take(2, grad_halo)
        grad_plane(grad_halo[side], far_place)
        input_terms(far_place, False)
        for row in range(rows):
            plane[pl.ds(row, channels, stride=rows), :] = total[:, row * lanes : (row + 1) * lanes]
        back = plane[0 : channels * rows, :].reshape(channels, rows, lanes)
        act = pre_ref[...].astype(jnp.float32)
        grad_in_ref[...] = (back * jnp.where(act > 0, 1.0, slope)).astype(grad_in_ref.dtype)

    waiting = list(sent)
    if orders:
        piece = (partial.shape[0] - 8) // (space_count * batch_count)
        partial[partial.shape[0] - 8 :, :] = jnp.zeros((8, lanes), jnp.float32)
        per_chunk = len(stage_refs) // len(orders)
        chunks, first_row = [], 0
        for number, order in enumerate(orders):
            refs = stage_refs[number * per_chunk : (number + 1) * per_chunk]
            chunks.append((order, refs[0], refs[1:], first_row, refs[0].shape[-2]))
            first_row += refs[0].shape[-2]

        def pack(order, held, first_row, count):
            for s in range(space_count):
                for b in range(batch_count):
                    start = (s * batch_count + b) * piece + first_row
                    place = dict(c=b % 2, z=b // 2, x=s % 2, y=s // 2)
                    index = tuple(place[axis] for axis in order)
                    held[index] = partial[start : start + count, :]

        def source_of(chunk, number):
            return chunk[1] if number == 0 else chunk[2][4 * number - 3]

        def begin(chunk, number):
            axis = chunk[0][number]
            received, _, send_sem, recv_sem = chunk[2][4 * number : 4 * number + 4]
            copies = []
            for step in range(1, extents[axis]):
                place = lax.rem(coords[axis] + step, extents[axis])
                copy = pltpu.make_async_remote_copy(
                    src_ref=source_of(chunk, number).at[place],
                    dst_ref=received.at[step - 1],
                    send_sem=send_sem.at[step - 1],
                    recv_sem=recv_sem.at[step - 1],
                    device_id=peer(axis, place),
                    device_id_type=MESH,
                )
                copy.start()
                copies.append(copy)
            waiting.extend(copies)
            return copies

        def end(chunk, number, copies):
            received, summed = chunk[2][4 * number : 4 * number + 2]
            value = source_of(chunk, number)[coords[chunk[0][number]]]
            for step, copy in enumerate(copies):
                copy.wait_recv()
                value = value + received[step]
            if number < 3:
                summed[...] = value
            else:
                weight_grad_ref[chunk[3] : chunk[3] + chunk[4], :] = value

        flights = []
        for chunk in chunks:
            pack(chunk[0], chunk[1], chunk[3], chunk[4])
            flights.append(begin(chunk, 0))
        pass_on(2)
        for number in range(1, 4):
            for place, chunk in enumerate(chunks):
                end(chunk, number - 1, flights[place])
                flights[place] = begin(chunk, number)
            if number == 1:
                input_terms(1, True)
            elif number == 2:
                pass_on(3)
                near_input()
            else:
                far_input()
        for place, chunk in enumerate(chunks):
            end(chunk, 3, flights[place])
    else:
        pass_on(2)
        pass_on(3)
        input_terms(1, True)
        near_input()
        far_input()
        weight_grad_ref[...] = partial[...]

    for copy in waiting:
        copy.wait_send()

    @pl.when(passes)
    def _():
        for index in range(4):
            passed(index).wait_send()


def fused_device(pre_act, grad_out, weight):
    samples, channels, local_x, rows, lanes = pre_act.shape
    out_chan, taps = grad_out.shape[1], weight.shape[0]
    space_count, batch_count = lax.axis_size("space"), lax.axis_size("batch")
    fits = (
        samples == 1
        and local_x == 1
        and taps == 27
        and rows == 8
        and lanes == 128
        and out_chan == 128
        and channels % 16 == 0
        and space_count % 2 == 0
    )
    if not fits:
        return on_device(pre_act, grad_out, weight)
    count = samples * batch_count * local_x * space_count * rows * lanes
    factor = 1.0 / count**0.5
    devices = space_count * batch_count
    total_rows = taps * channels
    scatter = (
        space_count > 2 and batch_count % 2 == 0 and batch_count > 2 and total_rows % devices == 0
        and total_rows // devices > 8
    )
    cells = rows * lanes
    widest = max(channels, out_chan)
    bf16, f32 = jnp.bfloat16, jnp.float32
    scratch = [
        pltpu.VMEM((channels, rows, lanes), bf16),
        pltpu.VMEM((out_chan, rows, lanes), bf16),
        pltpu.VMEM((taps, channels, out_chan), bf16),
        pltpu.VMEM((2, channels, rows, lanes), bf16),
        pltpu.VMEM((2, out_chan, rows, lanes), bf16),
        pltpu.VMEM((widest * rows, lanes), f32),
        pltpu.VMEM((3, 3 * channels, cells + 2 * lanes), bf16),
        pltpu.VMEM((3, 3 * out_chan, cells + 2 * lanes), bf16),
        pltpu.VMEM((channels, cells), f32),
        pltpu.VMEM((total_rows + 8 if scatter else total_rows, out_chan), f32),
        *[pltpu.SemaphoreType.DMA((4,))] * 5,
    ]
    owned, orders = total_rows, ()
    if scatter:
        piece = total_rows // devices
        owned = -(-piece // 8) * 8
        extents = dict(c=2, x=2, y=space_count // 2, z=batch_count // 2)
        tiles = owned // 8
        orders = ("cxyz", "cyxz") * min(2, tiles // 2)
        shares = [tiles // len(orders) + (n < tiles % len(orders)) for n in range(len(orders))]
        for order, count in zip(orders, [8 * share for share in shares]):
            sizes = [extents[axis] for axis in order]
            scratch.append(pltpu.VMEM((*sizes, count, out_chan), f32))
            for number, extent in enumerate(sizes):
                rest = (*sizes[number + 1 :], count, out_chan)
                scratch += [
                    pltpu.VMEM((extent - 1, *rest), f32),
                    pltpu.VMEM(rest, f32),
                    pltpu.SemaphoreType.DMA((extent - 1,)),
                    pltpu.SemaphoreType.DMA((extent - 1,)),
                ]
    vmem = pl.BlockSpec(memory_space=pltpu.VMEM)
    grad_in, weight_grad = pl.pallas_call(
        functools.partial(kernel, (space_count, batch_count), factor, orders),
        out_shape=(
            jax.ShapeDtypeStruct((channels, rows, lanes), bf16),
            jax.ShapeDtypeStruct((owned, out_chan), f32),
        ),
        in_specs=[pl.BlockSpec(memory_space=pltpu.HBM)] * 3,
        out_specs=(vmem, vmem),
        scratch_shapes=scratch,
        compiler_params=pltpu.CompilerParams(
            collective_id=0, has_side_effects=True, vmem_limit_bytes=48 * 2**20
        ),
    )(
        pltpu.with_memory_space_constraint(pre_act.reshape(channels, rows, lanes), pltpu.HBM),
        pltpu.with_memory_space_constraint(grad_out.reshape(out_chan, rows, lanes), pltpu.HBM),
        pltpu.with_memory_space_constraint(weight, pltpu.HBM),
    )
    grad_in = grad_in.reshape(pre_act.shape)
    if scatter:
        return grad_in, weight_grad[:piece].reshape(-1)
    space_part = lax.psum_scatter(
        weight_grad.reshape(-1), "space", scatter_dimension=0, tiled=True
    )
    return grad_in, lax.psum_scatter(space_part, "batch", scatter_dimension=0, tiled=True)


def solution(mesh):
    return jax.shard_map(
        fused_device,
        mesh=mesh,
        in_specs=(
            P("batch", None, "space", None, None),
            P("batch", None, "space", None, None),
            P(),
        ),
        out_specs=(P("batch", None, "space", None, None), P(("space", "batch"))),
        check_vma=False,
    )
```

```python
import functools

import jax
import jax.numpy as jnp
from jax import lax
from jax.experimental import pallas as pl
from jax.experimental.pallas import tpu as pltpu
from jax.sharding import PartitionSpec as P

slope = 0.3


def padded(block, sides, width):
    for axis, dim in sides:
        count = lax.axis_size(axis)
        forward = [(i, i + 1) for i in range(count - 1)]
        backward = [(target, source) for source, target in forward]
        low = lax.ppermute(
            lax.slice_in_dim(block, block.shape[dim] - width, None, axis=dim), axis, forward
        )
        high = lax.ppermute(lax.slice_in_dim(block, 0, width, axis=dim), axis, backward)
        block = jnp.concatenate([low, block, high], axis=dim)
    return block


def leaky(values):
    return jnp.where(values > 0, values, slope * values)


def on_device(pre_act, grad_out, weight):
    local_x = pre_act.shape[2]
    local_y = pre_act.shape[3]
    local_z = pre_act.shape[4]
    count = (
        pre_act.shape[0]
        * lax.axis_size("batch")
        * local_x
        * lax.axis_size("space")
        * local_y
        * local_z
    )
    factor = 1.0 / jnp.sqrt(jnp.float32(count))
    act_float = pre_act.astype(jnp.float32)
    yz_pad = ((0, 0), (0, 0), (0, 0), (1, 1), (1, 1))
    grad_hidden = jnp.zeros(pre_act.shape, jnp.float32)
    tap_grads = []
    joined = jnp.concatenate([pre_act, grad_out], axis=1)
    widened = padded(joined, (("space", 2),), 1)
    in_chan = pre_act.shape[1]
    hidden_pad = jnp.pad(
        leaky(widened[:, :in_chan].astype(jnp.float32)).astype(jnp.bfloat16), yz_pad
    )
    grad_pad = jnp.pad(widened[:, in_chan:], yz_pad)
    for tap in range(27):
        shift_x = tap // 9 - 1
        shift_y = tap // 3 % 3 - 1
        shift_z = tap % 3 - 1
        window = grad_pad[
            :,
            :,
            1 - shift_x : 1 - shift_x + local_x,
            1 - shift_y : 1 - shift_y + local_y,
            1 - shift_z : 1 - shift_z + local_z,
        ]
        grad_hidden = grad_hidden + jnp.einsum(
            "ic,scxyz->sixyz", weight[tap], window, preferred_element_type=jnp.float32
        )
        moved = hidden_pad[
            :,
            :,
            1 + shift_x : 1 + shift_x + local_x,
            1 + shift_y : 1 + shift_y + local_y,
            1 + shift_z : 1 + shift_z + local_z,
        ]
        tap_grads.append(
            jnp.einsum("sixyz,scxyz->ic", moved, grad_out, preferred_element_type=jnp.float32)
        )
    grad_in = (grad_hidden * jnp.where(act_float > 0, 1.0, slope)).astype(jnp.bfloat16)
    partial_sum = (jnp.stack(tap_grads) * factor).reshape(-1)
    space_part = lax.psum_scatter(partial_sum, "space", scatter_dimension=0, tiled=True)
    weight_grad = lax.psum_scatter(space_part, "batch", scatter_dimension=0, tiled=True)
    return (grad_in, weight_grad)


MESH = pl.DeviceIdType.MESH


def prepare(values, scratch, target):
    channels, rows, lanes = values.shape
    scratch[0 : channels * rows, :] = values.reshape(channels * rows, lanes)
    lane = lax.broadcasted_iota(jnp.int32, (channels, lanes), 1)
    blank = jnp.zeros((3 * channels, lanes), target.dtype)
    target[:, 0:lanes] = blank
    target[:, (rows + 1) * lanes : (rows + 2) * lanes] = blank
    for row in range(rows):
        block = scratch[pl.ds(row, channels, stride=rows), :]
        before = jnp.where(lane == 0, 0.0, pltpu.roll(block, 1, 1))
        after = jnp.where(lane == lanes - 1, 0.0, pltpu.roll(block, lanes - 1, 1))
        for place, shifted in enumerate((before, block, after)):
            target[
                place * channels : (place + 1) * channels, (row + 1) * lanes : (row + 2) * lanes
            ] = shifted.astype(target.dtype)


def kernel(
    sizes,
    factor,
    orders,
    pre_hbm,
    grad_hbm,
    weight_hbm,
    grad_in_ref,
    weight_grad_ref,
    pre_ref,
    grad_ref,
    weight_ref,
    pre_halo,
    grad_halo,
    plane,
    hidden_rows,
    grad_rows,
    total,
    partial,
    local_sem,
    direct_send,
    direct_recv,
    passed_send,
    passed_recv,
    *stage_refs,
):
    space_count, batch_count = sizes
    space, batch = lax.axis_index("space"), lax.axis_index("batch")
    channels, rows, lanes = pre_ref.shape
    out_chan = grad_ref.shape[0]
    cells = rows * lanes

    coords = dict(c=lax.rem(batch, 2), z=batch // 2, x=lax.rem(space, 2), y=space // 2)
    extents = dict(c=2, z=batch_count // 2, x=2, y=space_count // 2)
    side = coords["x"]

    def peer(axis, place):
        moved = dict(coords, **{axis: place})
        return (moved["y"] * 2 + moved["x"], moved["z"] * 2 + moved["c"])

    local = [
        pltpu.make_async_copy(source, target, local_sem.at[place])
        for place, (source, target) in enumerate(
            ((grad_hbm, grad_ref), (pre_hbm, pre_ref), (weight_hbm, weight_ref))
        )
    ]
    for copy in local:
        copy.start()

    barrier = pltpu.get_barrier_semaphore()
    low, high = space >= 2, space < space_count - 2
    if orders:
        greeted = 0
        for axis, extent in extents.items():
            for step in range(1, extent):
                pl.semaphore_signal(
                    barrier,
                    inc=1,
                    device_id=peer(axis, lax.rem(coords[axis] + step, extent)),
                    device_id_type=MESH,
                )
                greeted += 1
        pl.semaphore_wait(barrier, greeted)
    else:
        pl.semaphore_signal(
            barrier, inc=1, device_id=peer("x", 1 - side), device_id_type=MESH
        )
        for there, condition in ((space - 2, low), (space + 2, high)):

            @pl.when(condition)
            def _():
                pl.semaphore_signal(barrier, inc=1, device_id=(there, batch), device_id_type=MESH)

        pl.semaphore_wait(barrier, 1 + jnp.where(low, 1, 0) + jnp.where(high, 1, 0))

    half, quarter = out_chan // 2, channels // 2
    messages = [
        (pre_hbm.at[0:quarter], lambda slot: pre_halo.at[slot, 0:quarter]),
        (pre_hbm.at[quarter:channels], lambda slot: pre_halo.at[slot, quarter:channels]),
        (grad_hbm.at[0:half], lambda slot: grad_halo.at[slot, 0:half]),
        (grad_hbm.at[half:out_chan], lambda slot: grad_halo.at[slot, half:out_chan]),
    ]
    near = 1 - side
    passes = jnp.where(side == 0, space < space_count - 2, space >= 2)
    gets = jnp.where(side == 0, space >= 2, space < space_count - 2)
    beyond = jnp.where(side == 0, space + 2, space - 2)

    def direct(index):
        source, slots = messages[index]
        return pltpu.make_async_remote_copy(
            src_ref=source,
            dst_ref=slots(side),
            send_sem=direct_send.at[index],
            recv_sem=direct_recv.at[index],
            device_id=peer("x", 1 - side),
            device_id_type=MESH,
        )

    def passed(index):
        slots = messages[index][1]
        return pltpu.make_async_remote_copy(
            src_ref=slots(near),
            dst_ref=slots(side),
            send_sem=passed_send.at[index],
            recv_sem=passed_recv.at[index],
            device_id=(beyond, batch),
            device_id_type=MESH,
        )

    sent = [direct(index) for index in range(4)]
    for copy in sent:
        copy.start()

    def pass_on(index):
        sent[index].wait_recv()

        @pl.when(passes)
        def _():
            passed(index).start()

    def take(first, target):
        @pl.when(gets)
        def _():
            passed(first).wait_recv()
            passed(first + 1).wait_recv()

        @pl.when(jnp.logical_not(gets))
        def _():
            target[side] = jnp.zeros(target.shape[1:], target.dtype)

    def hidden_plane(values, place):
        prepare(leaky(values.astype(jnp.float32)), plane, hidden_rows.at[place])

    def grad_plane(values, place):
        prepare(values.astype(jnp.float32), plane, grad_rows.at[place])

    def weight_terms(place):
        own = grad_rows[1, out_chan : 2 * out_chan, lanes : lanes + cells]
        for shift_y in (-1, 0, 1):
            start = (9 * place + 3 * (shift_y + 1)) * channels
            if not isinstance(place, int):
                start = pl.multiple_of(start, 8)
            term = lax.dot_general(
                hidden_rows[place, :, (1 + shift_y) * lanes : (1 + shift_y) * lanes + cells],
                own,
                (((1,), (1,)), ((), ())),
                preferred_element_type=jnp.float32,
            )
            partial[pl.ds(start, 3 * channels), :] = term * factor

    def input_terms(place, first):
        for shift_y in (-1, 0, 1):
            tap = 9 * (2 - place) + 3 * (shift_y + 1)
            term = jnp.dot(
                jnp.concatenate([weight_ref[tap + 2], weight_ref[tap + 1], weight_ref[tap]], axis=1),
                grad_rows[place, :, (1 - shift_y) * lanes : (1 - shift_y) * lanes + cells],
                preferred_element_type=jnp.float32,
            )
            if first and shift_y == -1:
                total[...] = term
            else:
                total[...] += term

    near_place, far_place = 2 * near, 2 * side

    local[0].wait()
    local[1].wait()
    grad_plane(grad_ref[...], 1)
    hidden_plane(pre_ref[...], 1)
    pass_on(0)
    pass_on(1)
    weight_terms(1)
    hidden_plane(pre_halo[near], near_place)
    weight_terms(near_place)
    local[2].wait()
    take(0, pre_halo)
    hidden_plane(pre_halo[side], far_place)
    weight_terms(far_place)

    def near_input():
        grad_plane(grad_halo[near], near_place)
        input_terms(near_place, False)

    def far_input():
        take(2, grad_halo)
        grad_plane(grad_halo[side], far_place)
        input_terms(far_place, False)
        for row in range(rows):
            plane[pl.ds(row, channels, stride=rows), :] = total[:, row * lanes : (row + 1) * lanes]
        back = plane[0 : channels * rows, :].reshape(channels, rows, lanes)
        act = pre_ref[...].astype(jnp.float32)
        grad_in_ref[...] = (back * jnp.where(act > 0, 1.0, slope)).astype(grad_in_ref.dtype)

    waiting = list(sent)
    if orders:
        piece = (partial.shape[0] - 8) // (space_count * batch_count)
        partial[partial.shape[0] - 8 :, :] = jnp.zeros((8, lanes), jnp.float32)
        per_chunk = len(stage_refs) // len(orders)
        chunks, first_row = [], 0
        for number, order in enumerate(orders):
            refs = stage_refs[number * per_chunk : (number + 1) * per_chunk]
            chunks.append((order, refs[0], refs[1:], first_row, refs[0].shape[-2]))
            first_row += refs[0].shape[-2]

        def pack(order, held, first_row, count):
            for s in range(space_count):
                for b in range(batch_count):
                    start = (s * batch_count + b) * piece + first_row
                    place = dict(c=b % 2, z=b // 2, x=s % 2, y=s // 2)
                    index = tuple(place[axis] for axis in order)
                    held[index] = partial[start : start + count, :]

        def source_of(chunk, number):
            return chunk[1] if number == 0 else chunk[2][4 * number - 3]

        def begin(chunk, number):
            axis = chunk[0][number]
            received, _, send_sem, recv_sem = chunk[2][4 * number : 4 * number + 4]
            copies = []
            for step in range(1, extents[axis]):
                place = lax.rem(coords[axis] + step, extents[axis])
                copy = pltpu.make_async_remote_copy(
                    src_ref=source_of(chunk, number).at[place],
                    dst_ref=received.at[step - 1],
                    send_sem=send_sem.at[step - 1],
                    recv_sem=recv_sem.at[step - 1],
                    device_id=peer(axis, place),
                    device_id_type=MESH,
                )
                copy.start()
                copies.append(copy)
            waiting.extend(copies)
            return copies

        def end(chunk, number, copies):
            received, summed = chunk[2][4 * number : 4 * number + 2]
            value = source_of(chunk, number)[coords[chunk[0][number]]]
            for step, copy in enumerate(copies):
                copy.wait_recv()
                value = value + received[step]
            if number < 3:
                summed[...] = value
            else:
                weight_grad_ref[chunk[3] : chunk[3] + chunk[4], :] = value

        flights = []
        for chunk in chunks:
            pack(chunk[0], chunk[1], chunk[3], chunk[4])
            flights.append(begin(chunk, 0))
        for number in range(1, 4):
            for place, chunk in enumerate(chunks):
                end(chunk, number - 1, flights[place])
                flights[place] = begin(chunk, number)
            if number == 1:
                pass_on(2)
                input_terms(1, True)
            elif number == 2:
                pass_on(3)
                near_input()
            else:
                far_input()
        for place, chunk in enumerate(chunks):
            end(chunk, 3, flights[place])
    else:
        pass_on(2)
        pass_on(3)
        input_terms(1, True)
        near_input()
        far_input()
        weight_grad_ref[...] = partial[...]

    for copy in waiting:
        copy.wait_send()

    @pl.when(passes)
    def _():
        for index in range(4):
            passed(index).wait_send()


def fused_device(pre_act, grad_out, weight):
    samples, channels, local_x, rows, lanes = pre_act.shape
    out_chan, taps = grad_out.shape[1], weight.shape[0]
    space_count, batch_count = lax.axis_size("space"), lax.axis_size("batch")
    fits = (
        samples == 1
        and local_x == 1
        and taps == 27
        and rows == 8
        and lanes == 128
        and out_chan == 128
        and channels % 16 == 0
        and space_count % 2 == 0
    )
    if not fits:
        return on_device(pre_act, grad_out, weight)
    count = samples * batch_count * local_x * space_count * rows * lanes
    factor = 1.0 / count**0.5
    devices = space_count * batch_count
    total_rows = taps * channels
    scatter = (
        space_count > 2 and batch_count % 2 == 0 and batch_count > 2 and total_rows % devices == 0
        and total_rows // devices > 8
    )
    cells = rows * lanes
    widest = max(channels, out_chan)
    bf16, f32 = jnp.bfloat16, jnp.float32
    scratch = [
        pltpu.VMEM((channels, rows, lanes), bf16),
        pltpu.VMEM((out_chan, rows, lanes), bf16),
        pltpu.VMEM((taps, channels, out_chan), bf16),
        pltpu.VMEM((2, channels, rows, lanes), bf16),
        pltpu.VMEM((2, out_chan, rows, lanes), bf16),
        pltpu.VMEM((widest * rows, lanes), f32),
        pltpu.VMEM((3, 3 * channels, cells + 2 * lanes), bf16),
        pltpu.VMEM((3, 3 * out_chan, cells + 2 * lanes), bf16),
        pltpu.VMEM((channels, cells), f32),
        pltpu.VMEM((total_rows + 8 if scatter else total_rows, out_chan), f32),
        *[pltpu.SemaphoreType.DMA((4,))] * 5,
    ]
    owned, orders = total_rows, ()
    if scatter:
        piece = total_rows // devices
        owned = -(-piece // 8) * 8
        extents = dict(c=2, x=2, y=space_count // 2, z=batch_count // 2)
        tiles = owned // 8
        orders = ("cxyz", "cyxz") * min(2, tiles // 2)
        shares = [tiles // len(orders) + (n < tiles % len(orders)) for n in range(len(orders))]
        for order, count in zip(orders, [8 * share for share in shares]):
            sizes = [extents[axis] for axis in order]
            scratch.append(pltpu.VMEM((*sizes, count, out_chan), f32))
            for number, extent in enumerate(sizes):
                rest = (*sizes[number + 1 :], count, out_chan)
                scratch += [
                    pltpu.VMEM((extent - 1, *rest), f32),
                    pltpu.VMEM(rest, f32),
                    pltpu.SemaphoreType.DMA((extent - 1,)),
                    pltpu.SemaphoreType.DMA((extent - 1,)),
                ]
    vmem = pl.BlockSpec(memory_space=pltpu.VMEM)
    grad_in, weight_grad = pl.pallas_call(
        functools.partial(kernel, (space_count, batch_count), factor, orders),
        out_shape=(
            jax.ShapeDtypeStruct((channels, rows, lanes), bf16),
            jax.ShapeDtypeStruct((owned, out_chan), f32),
        ),
        in_specs=[pl.BlockSpec(memory_space=pltpu.HBM)] * 3,
        out_specs=(vmem, vmem),
        scratch_shapes=scratch,
        compiler_params=pltpu.CompilerParams(
            collective_id=0, has_side_effects=True, vmem_limit_bytes=48 * 2**20
        ),
    )(
        pltpu.with_memory_space_constraint(pre_act.reshape(channels, rows, lanes), pltpu.HBM),
        pltpu.with_memory_space_constraint(grad_out.reshape(out_chan, rows, lanes), pltpu.HBM),
        pltpu.with_memory_space_constraint(weight, pltpu.HBM),
    )
    grad_in = grad_in.reshape(pre_act.shape)
    if scatter:
        return grad_in, weight_grad[:piece].reshape(-1)
    space_part = lax.psum_scatter(
        weight_grad.reshape(-1), "space", scatter_dimension=0, tiled=True
    )
    return grad_in, lax.psum_scatter(space_part, "batch", scatter_dimension=0, tiled=True)


def solution(mesh):
    return jax.shard_map(
        fused_device,
        mesh=mesh,
        in_specs=(
            P("batch", None, "space", None, None),
            P("batch", None, "space", None, None),
            P(),
        ),
        out_specs=(P("batch", None, "space", None, None), P(("space", "batch"))),
        check_vma=False,
    )
```
